32 devices in a mesh: seq: 8 (over z, x), head: 4 (over y, core).
Axes of the slice: x: 2, y: 2, z: 4, core: 2. Of those that a mesh axis runs over, the one named last changes fastest.
Arguments:
- tokens: bfloat16 [16384, 768], P(('seq', 'head')), may hold values from -6 to 6
- out_grad: bfloat16 [16384, 768], P(('seq', 'head')), may hold values from -6 to 6
- seq_lengths: int32 [8], replicated, may hold values from 1024 to 2048, as said below
- dispatch_order: int32 [8], replicated, may hold values from 0 to 7, as said below
- random_key_blocks: int32 [8, 32, 3], replicated, may hold values from 0 to 31
- qkv_proj: bfloat16 [768, 2304], P('seq'), may hold values from -0.21875 to 0.21875
- attn_proj: bfloat16 [768, 768], P('seq'), may hold values from -3.5 to 3.5
- up_proj: bfloat16 [768, 3072], P('seq'), may hold values from -0.21875 to 0.21875
- up_bias: bfloat16 [3072], P('seq'), may hold values from -3 to 3
- down_proj: bfloat16 [3072, 768], P('seq'), may hold values from -0.109375 to 0.109375
- down_bias: bfloat16 [768], P('seq'), may hold values from -3 to 3
- norm1_gain: bfloat16 [768], P('seq'), may hold values from 0.5 to 2
- norm1_bias: bfloat16 [768], P('seq'), may hold values from -3 to 3
- norm2_gain: bfloat16 [768], P('seq'), may hold values from 0.5 to 2
- norm2_bias: bfloat16 [768], P('seq'), may hold values from -3 to 3
Outputs:
- output: bfloat16 [16384, 768], P(('seq', 'head'))
- grad_tokens: bfloat16 [16384, 768], P(('seq', 'head'))
- grad_qkv_proj: float32 [768, 2304], P('seq')
- grad_attn_proj: float32 [768, 768], P('seq')
- grad_up_proj: float32 [768, 3072], P('seq')
- grad_up_bias: float32 [3072], P('seq')
- grad_down_proj: float32 [3072, 768], P('seq')
- grad_down_bias: float32 [768], P('seq')
- grad_norm1_gain: float32 [768], P('seq')
- grad_norm1_bias: float32 [768], P('seq')
- grad_norm2_gain: float32 [768], P('seq')
- grad_norm2_bias: float32 [768], P('seq')
The draws below stay inside these ranges and needn't reach their ends.
Inputs may be any that keep to these rules, and one draw needn't show every extreme that they name: `seq_lengths`: one slot has length exactly 2048 and another exactly 1024. `dispatch_order`: A permutation of the slots.
All inputs are finite; a program needn't handle non-finite values.
Results may differ from the reference program's by a relative error of at most 0.017.
Values may be sent and summed in bfloat16 or wider, within the bound.
No kernel may reach another device: no remote copies, remote signals or barrier semaphores. Data moves between devices by JAX's collectives and lax.ppermute only.
A program may use at most 128 MiB of HBM per device.

```python
import math
import jax
import jax.numpy as jnp
from jax import lax

D = 768
H = 12
HD = 64
FF = 3072
BLOCK_TOKENS = 64
RANDOM_KEYS = 3
SLOT_TOKENS = 2048
SLOT_BLOCKS = 32
SEQUENCE_COUNT = 8
TOKENS = 16384
N_SEQ = 8


def draw_seq_lengths(key, part):
    slot_total = N_SEQ
    lengths = jax.random.randint(jax.random.fold_in(key, 11), (slot_total,), SLOT_TOKENS // 2, SLOT_TOKENS + 1)
    chosen = jax.random.permutation(jax.random.fold_in(key, 12), slot_total)
    lengths = lengths.at[chosen[0]].set(SLOT_TOKENS).at[chosen[1]].set(SLOT_TOKENS // 2)
    return lengths.astype(jnp.int32)


def draw_dispatch_order(key, part):
    return jax.random.permutation(jax.random.fold_in(key, 13), N_SEQ).astype(jnp.int32)


def with_ends(values, key, low, high):
    extent = values.shape
    place = [jax.random.randint(jax.random.fold_in(key, axis), (), 0, extent[axis]) for axis in range(len(extent))]
    values = values.at[tuple(place)].set(low)
    longest = extent.index(max(extent))
    place[longest] = (place[longest] + 1) % extent[longest]
    return values.at[tuple(place)].set(high)


def with_spikes(entries, stream_key, source, target, shards_of, factor):
    def block_of(dim):
        return (jnp.arange(entries.shape[dim]) // (entries.shape[dim] // shards_of)).reshape((-1,) + (1,) * (entries.ndim - 1 - dim))

    first = jax.random.permutation(stream_key, shards_of)[block_of(target)]
    second = (block_of(target) + shards_of // 2) % shards_of
    return jnp.where((block_of(source) == first) | (block_of(source) == second), factor * entries, entries)


def shard_levels(stream_key, extent, split, low, largest):
    factor_of, own = 1.0, jax.random.fold_in(stream_key, 6)
    for dim, blocks in split:
        draws = jnp.exp(jax.random.uniform(jax.random.fold_in(own, dim), (blocks,), jnp.float32, low / len(split), largest / len(split)))
        factor_of = factor_of * jnp.repeat(draws, extent[dim] // blocks).reshape([-1 if axis == dim else 1 for axis in range(len(extent))])
    return factor_of


def scatter_about(own_key, dims, spread, limit, split=(), dtype=jnp.bfloat16):
    values = jax.random.normal(own_key, dims, jnp.float32) * spread
    if len(split) > 0:
        values = shard_levels(own_key, dims, split, -0.22, 0.18) * values
    return jnp.clip(values, min=-limit, max=limit).astype(dtype)


def bell_draw_with(key, shape, spread, bound, shards, heavy, kind=jnp.bfloat16):
    drawn = spread * jax.random.normal(key, shape, jnp.float32)
    if shards:
        drawn = drawn * shard_levels(key, shape, shards, -0.22, 0.18)
    return jnp.clip(with_spikes(drawn, jax.random.fold_in(key, 3), *heavy), -bound, bound).astype(kind)


def setup_inputs(seed: int = 0) -> dict:
    arg_keys = jax.random.split(jax.random.key(seed), 16)
    return {
        "tokens": bell_draw_with(arg_keys[0], (TOKENS, D), 1.0, 6.0, ((0, 32),), (0, 1, 32, 2.75)),
        "out_grad": scatter_about(arg_keys[1], (TOKENS, D), 1.0, 6.0, ((0, 32),)),
        "seq_lengths": draw_seq_lengths(jax.random.fold_in(arg_keys[15], 71), 0),
        "dispatch_order": draw_dispatch_order(jax.random.fold_in(arg_keys[15], 71), 0),
        "random_key_blocks": with_ends(jax.random.randint(arg_keys[4], (SEQUENCE_COUNT, SLOT_BLOCKS, RANDOM_KEYS), 0, SLOT_TOKENS // BLOCK_TOKENS), jax.random.fold_in(arg_keys[4], 1), 0, (SLOT_TOKENS // BLOCK_TOKENS) - 1).astype(jnp.int32),
        "qkv_proj": scatter_about(arg_keys[5], (D, 3 * D), D ** -0.5, 0.21875, ((0, 8),)),
        "attn_proj": scatter_about(arg_keys[6], (D, D), (max(D // 256, 1)) ** -0.5, 3.5, ((0, 8),)),
        "up_proj": scatter_about(arg_keys[7], (D, FF), D ** -0.5, 0.21875, ((0, 8),)),
        "up_bias": scatter_about(arg_keys[8], (FF,), 0.5, 3.0, ((0, 8),)),
        "down_proj": scatter_about(arg_keys[9], (FF, D), FF ** -0.5, 0.109375, ((0, 8),)),
        "down_bias": scatter_about(arg_keys[10], (D,), 0.5, 3.0, ((0, 8),)),
        "norm1_gain": jnp.clip(jnp.exp(math.log(2.0) - 1.3862944 * jax.random.uniform(arg_keys[11], (D,), jnp.float32) ** shard_levels(arg_keys[11], (D,), ((0, 8),), -0.2, 0.2)), 0.5, 2.0).astype(jnp.bfloat16),
        "norm1_bias": scatter_about(arg_keys[12], (D,), 0.5, 3.0, ((0, 8),)),
        "norm2_gain": jnp.clip(jnp.exp(math.log(2.0) - 1.3862944 * jax.random.uniform(arg_keys[13], (D,), jnp.float32) ** shard_levels(arg_keys[13], (D,), ((0, 8),), -0.2, 0.2)), 0.5, 2.0).astype(jnp.bfloat16),
        "norm2_bias": scatter_about(arg_keys[14], (D,), 0.5, 3.0, ((0, 8),)),
    }


@jax.custom_vjp
def low(v):
    return lax.optimization_barrier(v.astype(jnp.bfloat16)).astype(jnp.float32)

@jax.custom_vjp
def low_back(v):
    return v

def low_keep(v):
    return (low(v), None)

def low_pass(kept, grad):
    return (grad,)

def back_keep(v):
    return (v, None)

def back_low(kept, grad):
    return (low(grad),)
low.defvjp(low_keep, low_pass)
low_back.defvjp(back_keep, back_low)
highest = lax.Precision.HIGHEST
eps_norm = 1e-12

def matmul(left, right):
    return jnp.dot(left, right, precision=highest, preferred_element_type=jnp.float32)

def layer_norm(hidden, norm_gain, norm_shift):
    center = hidden - lax.optimization_barrier(jnp.mean(hidden, axis=-1, keepdims=True))
    variance = lax.optimization_barrier(jnp.mean(center * center, axis=-1, keepdims=True))
    return center * lax.rsqrt(variance + eps_norm) * norm_gain + norm_shift

def token_mask(blocks, length, slot_size):
    block_count = slot_size // BLOCK_TOKENS
    block_rows = jnp.arange(block_count)[:, None]
    block_cols = jnp.arange(block_count)[None, :]
    last_block = (length - 1) // BLOCK_TOKENS
    picked = jnp.any(blocks[:, :, None] == jnp.arange(block_count)[None, None, :], axis=1)
    allowed = (jnp.abs(block_rows - block_cols) <= 1) | (block_rows == 0) | (block_cols == 0) | (block_rows == last_block) | (block_cols == last_block) | picked
    expanded = jnp.repeat(jnp.repeat(allowed, BLOCK_TOKENS, axis=0), BLOCK_TOKENS, axis=1)
    places = jnp.arange(slot_size)
    return (expanded & (places[None, :] < length), places < length)

def attend(queries, keys_in, values_in, length, blocks):
    allowed_mask, query_valid = token_mask(blocks, length, queries.shape[0])
    valid_float = query_valid[:, None].astype(jnp.float32)

    def one_head(head_item):
        head_q, head_k, head_v = head_item
        raw_scores = matmul(head_q, head_k.T)
        scores = low_back(raw_scores) * HD ** (-0.5)
        masked = jnp.where(allowed_mask, scores, -1e+30)
        row_max = lax.optimization_barrier(jnp.max(masked, axis=-1, keepdims=True))
        weights_exp = jnp.where(allowed_mask, jnp.exp(masked - row_max), 0.0)
        attn_probs = weights_exp / lax.optimization_barrier(jnp.sum(weights_exp, axis=-1, keepdims=True))
        attn_probs = attn_probs * valid_float
        return matmul(low(attn_probs), head_v)
    per_head = lax.map(jax.checkpoint(one_head), (queries.transpose(1, 0, 2), keys_in.transpose(1, 0, 2), values_in.transpose(1, 0, 2)))
    attended = per_head.transpose(1, 0, 2)
    return low_back(low(attended))

def slot_layer(param_list, slot_rows, length, blocks):
    qkv_w, attn_w, up_w, up_b, down_w, down_b, gain_one, shift_one, gain_two, shift_two = param_list
    slot_size = slot_rows.shape[0]
    packed = low_back(low(matmul(slot_rows, qkv_w))).reshape(slot_size, 3, H, HD)
    head_mixed = attend(packed[:, 0], packed[:, 1], packed[:, 2], length, blocks).reshape(slot_size, D)
    attn_term = low_back(matmul(head_mixed, attn_w))
    first_norm = layer_norm(slot_rows + attn_term, gain_one, shift_one)
    up_pre = low_back(matmul(low(first_norm), up_w)) + up_b
    act_low = low(jax.nn.gelu(up_pre, approximate=True))
    down_term = low_back(matmul(act_low, down_w))
    return layer_norm(first_norm + down_term + down_b, gain_two, shift_two)

def reference(tokens, out_grad, seq_lengths, dispatch_order, random_key_blocks, qkv_proj, attn_proj, up_proj, up_bias, down_proj, down_bias, norm1_gain, norm1_bias, norm2_gain, norm2_bias):
    param_list = tuple((item.astype(jnp.float32) for item in (qkv_proj, attn_proj, up_proj, up_bias, down_proj, down_bias, norm1_gain, norm1_bias, norm2_gain, norm2_bias)))
    slot_total = N_SEQ
    slot_rows = tokens.astype(jnp.float32).reshape(slot_total, SLOT_TOKENS, D)
    position = jnp.argsort(dispatch_order).astype(jnp.int32)
    blocks = random_key_blocks[position]
    lengths = seq_lengths

    def forward(params_in, rows_in):

        def slot_step(slot_item):
            return slot_layer(params_in, slot_item[0], slot_item[1], slot_item[2])
        return lax.map(jax.checkpoint(slot_step), (rows_in, lengths, blocks))
    result, pullback = jax.vjp(forward, param_list, slot_rows)
    grad_list, grad_rows = pullback(out_grad.astype(jnp.float32).reshape(slot_rows.shape))
    return (result.reshape(-1, D).astype(jnp.bfloat16), grad_rows.reshape(-1, D).astype(jnp.bfloat16), grad_list[0], grad_list[1], grad_list[2], grad_list[3], grad_list[4], grad_list[5], grad_list[6], grad_list[7], grad_list[8], grad_list[9])
```

```python
from functools import partial

import jax
import jax.numpy as jnp
from jax import lax
from jax.experimental import pallas as pl
from jax.experimental.pallas import tpu as pltpu
from jax.sharding import PartitionSpec as P

H = 12
HD = 64
BLOCK_TOKENS = 64
RANDOM_KEYS = 3
KEY_BLOCKS = 5 + RANDOM_KEYS
STEPS = 4
F32 = jnp.float32
BF16 = jnp.bfloat16
LAST_LAST = (((1,), (1,)), ((), ()))
FIRST_FIRST = (((0,), (0,)), ((), ()))


eps_norm = 1e-12


def layer_norm(hidden, norm_gain, norm_shift):
    center = hidden - jnp.mean(hidden, axis=-1, keepdims=True)
    variance = jnp.mean(center * center, axis=-1, keepdims=True)
    return center * lax.rsqrt(variance + eps_norm) * norm_gain + norm_shift


def key_blocks(i, last, length, picks_ref, block_count):
    live = (i > 0) & (i < last)
    chosen = [jnp.maximum(i - 1, 0), i, jnp.minimum(i + 1, block_count - 1), 0 * i, last]
    chosen += [picks_ref[i * RANDOM_KEYS + r] for r in range(RANDOM_KEYS)]
    limits = []
    for c, j in enumerate(chosen):
        counts = live & (j <= last)
        for earlier in chosen[:c]:
            counts = counts & (j != earlier)
        limits.append(jnp.where(counts, jnp.minimum(length - j * BLOCK_TOKENS, BLOCK_TOKENS), 0))
    return live, chosen, limits


def key_bias(limits):
    lane = lax.broadcasted_iota(jnp.int32, (1, KEY_BLOCKS * BLOCK_TOKENS), 1)
    seen = jnp.zeros((1, KEY_BLOCKS * BLOCK_TOKENS), jnp.int32)
    for c, limit in enumerate(limits):
        start = c * BLOCK_TOKENS
        seen = jnp.where((lane >= start) & (lane < start + limit), 1, seen)
    return jnp.where(seen == 1, 0.0, -1e30).astype(F32)


def spread(rows, heads):
    lane = lax.broadcasted_iota(jnp.int32, rows.shape, 1)
    parts = [
        jnp.where((lane >= n * HD) & (lane < (n + 1) * HD), rows, jnp.zeros_like(rows))
        for n in range(heads)
    ]
    return jnp.concatenate(parts, axis=0)


def fold(full, heads):
    count = full.shape[0] // heads
    lane = lax.broadcasted_iota(jnp.int32, (count, full.shape[1]), 1)
    rows = full[:count]
    for n in range(1, heads):
        rows = jnp.where(lane >= n * HD, full[n * count : (n + 1) * count], rows)
    return rows


def block_at(j, flip):
    return pl.ds(pl.multiple_of((j ^ flip) * BLOCK_TOKENS, BLOCK_TOKENS), BLOCK_TOKENS)


def take_blocks(ref, chosen, flip):
    return jnp.concatenate([ref[block_at(j, flip), :] for j in chosen], axis=0)


def attend_kernel(
    picks_ref, place_ref, q_ref, k_ref, v_ref, mixed_ref, probs_ref, edge_ref, *, heads, block_count
):
    step = pl.program_id(0)
    per_step = block_count // STEPS
    length, flip = place_ref[0], place_ref[1]
    last = (length - 1) // BLOCK_TOKENS

    def softmax(i, keys, bias):
        queries = q_ref[block_at(i, flip), :] * jnp.asarray(HD**-0.5, BF16)
        scores = lax.dot_general(
            spread(queries, heads), keys, LAST_LAST, preferred_element_type=F32
        )
        scores = scores + bias
        weights = jnp.exp(scores - jnp.max(scores, axis=-1, keepdims=True))
        return weights, jnp.sum(weights, axis=-1, keepdims=True)

    @pl.when(step == 0)
    def _():
        mixed_ref[...] = jnp.zeros_like(mixed_ref)

    def two_blocks(t, carry):
        found = []
        for u in range(2):
            i = step * per_step + 2 * t + u
            live, chosen, limits = key_blocks(i, last, length, picks_ref, block_count)
            weights, total = softmax(i, take_blocks(k_ref, chosen, flip), key_bias(limits))
            low = (weights * (jnp.where(live, 1.0, 0.0) / total)).astype(BF16)
            probs_ref[2 * t + u] = low
            mixed = jnp.dot(low, take_blocks(v_ref, chosen, flip), preferred_element_type=F32)
            found.append((i, fold(mixed, heads).astype(BF16)))
        for i, mixed in found:
            mixed_ref[block_at(i, flip), :] = mixed
        return carry

    count = jnp.maximum(jnp.minimum(per_step, last - step * per_step), 0)
    lax.fori_loop(0, (count + 1) // 2, two_blocks, 0)

    @pl.when(step == STEPS - 1)
    def _():
        slot_size = block_count * BLOCK_TOKENS
        place = lax.broadcasted_iota(jnp.int32, (1, slot_size), 1) ^ (flip * BLOCK_TOKENS)
        bias = jnp.where(place < length, 0.0, -1e30).astype(F32)

        def edge(n, carry):
            i = n * last
            weights, total = softmax(i, k_ref[...], bias)
            row = lax.broadcasted_iota(jnp.int32, (heads * BLOCK_TOKENS, 1), 0)
            valid = (row % BLOCK_TOKENS) + i * BLOCK_TOKENS < length
            low = (weights * (jnp.where(valid, 1.0, 0.0) / total)).astype(BF16)
            edge_ref[n] = low
            mixed = jnp.dot(low, v_ref[...], preferred_element_type=F32)
            mixed_ref[block_at(i, flip), :] = fold(mixed, heads).astype(BF16)
            return carry

        lax.fori_loop(0, jnp.minimum(last, 1) + 1, edge, 0)


def attend_back_kernel(
    picks_ref,
    place_ref,
    q_ref,
    k_ref,
    v_ref,
    grad_ref,
    probs_ref,
    edge_ref,
    dq_ref,
    dk_ref,
    dv_ref,
    key_total,
    value_total,
    *,
    heads,
    block_count,
):
    step = pl.program_id(0)
    per_step = block_count // STEPS
    length, flip = place_ref[0], place_ref[1]
    last = (length - 1) // BLOCK_TOKENS

    @pl.when(step == 0)
    def _():
        dq_ref[...] = jnp.zeros_like(dq_ref)
        key_total[...] = jnp.zeros_like(key_total)
        value_total[...] = jnp.zeros_like(value_total)

    def back(i, low, keys, values):
        at = block_at(i, flip)
        queries = spread(q_ref[at, :] * jnp.asarray(HD**-0.5, BF16), heads)
        grads = spread(grad_ref[at, :], heads)
        grad_probs = lax.dot_general(grads, values, LAST_LAST, preferred_element_type=F32)
        probs = low.astype(F32)
        inner = jnp.sum(probs * grad_probs, axis=-1, keepdims=True)
        grad_scores = (probs * (grad_probs - inner)).astype(BF16)
        dq = fold(jnp.dot(grad_scores, keys, preferred_element_type=F32), heads) * (HD**-0.5)
        dk = lax.dot_general(grad_scores, queries, FIRST_FIRST, preferred_element_type=F32)
        dv = lax.dot_general(low, grads, FIRST_FIRST, preferred_element_type=F32)
        return dq.astype(BF16), dk, dv

    def two_blocks(t, carry):
        found = []
        for u in range(2):
            i = step * per_step + 2 * t + u
            live, chosen, limits = key_blocks(i, last, length, picks_ref, block_count)
            keys, values = take_blocks(k_ref, chosen, flip), take_blocks(v_ref, chosen, flip)
            found.append((i, chosen) + back(i, probs_ref[2 * t + u], keys, values))
        for i, chosen, dq, dk, dv in found:
            dq_ref[block_at(i, flip), :] = dq
            for c, j in enumerate(chosen):
                rows = slice(c * BLOCK_TOKENS, (c + 1) * BLOCK_TOKENS)
                key_total[block_at(j, flip), :] += dk[rows]
                value_total[block_at(j, flip), :] += dv[rows]
        return carry

    count = jnp.maximum(jnp.minimum(per_step, last - step * per_step), 0)
    lax.fori_loop(0, (count + 1) // 2, two_blocks, 0)

    @pl.when(step == STEPS - 1)
    def _():
        def edge(n, carry):
            i = n * last
            dq, dk, dv = back(i, edge_ref[n], k_ref[...], v_ref[...])
            dq_ref[block_at(i, flip), :] = dq
            key_total[...] += dk
            value_total[...] += dv
            return carry

        lax.fori_loop(0, jnp.minimum(last, 1) + 1, edge, 0)
        dk_ref[...] = key_total[...].astype(BF16)
        dv_ref[...] = value_total[...].astype(BF16)


def whole(shape):
    return pl.BlockSpec(shape, lambda step, *_: (0,) * len(shape))


def probs_specs(heads, block_count):
    rows = heads * BLOCK_TOKENS
    span = KEY_BLOCKS * BLOCK_TOKENS
    slot_size = block_count * BLOCK_TOKENS
    shapes = [
        jax.ShapeDtypeStruct((block_count, rows, span), BF16),
        jax.ShapeDtypeStruct((2, rows, slot_size), BF16),
    ]
    specs = [
        pl.BlockSpec((block_count // STEPS, rows, span), lambda step, *_: (step, 0, 0)),
        whole((2, rows, slot_size)),
    ]
    return shapes, specs


def attend(queries, keys, values, picks, place):
    slot_size, span = queries.shape
    heads, block_count = span // HD, slot_size // BLOCK_TOKENS
    shapes, specs = probs_specs(heads, block_count)
    return pl.pallas_call(
        partial(attend_kernel, heads=heads, block_count=block_count),
        grid_spec=pltpu.PrefetchScalarGridSpec(
            num_scalar_prefetch=2,
            grid=(STEPS,),
            in_specs=[whole((slot_size, span))] * 3,
            out_specs=[whole((slot_size, span))] + specs,
        ),
        out_shape=[jax.ShapeDtypeStruct((slot_size, span), BF16)] + shapes,
        compiler_params=pltpu.CompilerParams(
            dimension_semantics=("arbitrary",), vmem_limit_bytes=48 << 20
        ),
        cost_estimate=pl.CostEstimate(
            flops=12 << 30, bytes_accessed=12 << 20, transcendentals=4 << 20
        ),
        name="attend",
    )(picks, place, queries, keys, values)


def attend_back(queries, keys, values, grads, probs, edge, picks, place):
    slot_size, span = queries.shape
    heads, block_count = span // HD, slot_size // BLOCK_TOKENS
    _, specs = probs_specs(heads, block_count)
    return pl.pallas_call(
        partial(attend_back_kernel, heads=heads, block_count=block_count),
        grid_spec=pltpu.PrefetchScalarGridSpec(
            num_scalar_prefetch=2,
            grid=(STEPS,),
            in_specs=[whole((slot_size, span))] * 4 + specs,
            out_specs=[whole((slot_size, span))] * 3,
            scratch_shapes=[pltpu.VMEM((slot_size, span), F32)] * 2,
        ),
        out_shape=[jax.ShapeDtypeStruct((slot_size, span), BF16)] * 3,
        compiler_params=pltpu.CompilerParams(
            dimension_semantics=("arbitrary",), vmem_limit_bytes=48 << 20
        ),
        cost_estimate=pl.CostEstimate(
            flops=18 << 30, bytes_accessed=14 << 20, transcendentals=0
        ),
        name="attend_back",
    )(picks, place, queries, keys, values, grads, probs, edge)


def swap(values, axis, bits):
    size = lax.axis_size(axis)
    return lax.ppermute(values, axis, [(i, i ^ bits) for i in range(size)])


def seq_gather(piece):
    if lax.axis_size("seq") != 8:
        return lax.all_gather(piece, "seq")
    far = {k: swap(piece, "seq", k) for k in (4, 6, 2)}
    slots = [piece, swap(piece, "seq", 1)]
    for k in (2, 4, 6):
        slots += [far[k], swap(far[k], "seq", 1)]
    return jnp.take(jnp.stack(slots), jnp.arange(8) ^ lax.axis_index("seq"), axis=0)


def seq_reduce(chunks):
    if lax.axis_size("seq") != 8:
        return lax.psum_scatter(chunks, "seq", scatter_dimension=0).astype(F32)
    own = lax.axis_index("seq")

    def slot(k):
        return lax.dynamic_index_in_dim(chunks, own ^ k, 0, keepdims=False)

    near = {k: swap(slot(k + 1), "seq", 1) for k in (4, 6, 2, 0)}
    pairs = {k: slot(k).astype(F32) + near[k].astype(F32) for k in (4, 6, 2, 0)}
    far = [swap(pairs[k].astype(BF16), "seq", k) for k in (4, 6, 2)]
    return pairs[0] + sum(part.astype(F32) for part in far)


def head_gather(piece):
    across = swap(piece, "head", 2)
    beside = swap(piece, "head", 1)
    return [piece, beside, across, swap(across, "head", 1)]


def head_exchange(parts):
    sent = {k: swap(parts[k], "head", k) for k in (2, 3, 1)}
    return [parts[0], sent[1], sent[2], sent[3]]


def in_order(own, other, low_bit, axis):
    return jnp.where(low_bit == 0, jnp.stack([own, other], axis), jnp.stack([other, own], axis))


def on_device(
    tokens,
    out_grad,
    seq_lengths,
    dispatch_order,
    random_key_blocks,
    qkv_proj,
    attn_proj,
    up_proj,
    up_bias,
    down_proj,
    down_bias,
    norm1_gain,
    norm1_bias,
    norm2_gain,
    norm2_bias,
):
    seq_parts = lax.axis_size("seq")
    head_parts = lax.axis_size("head")
    seq_at = lax.axis_index("seq")
    head_at = lax.axis_index("head")
    side = head_at % 2
    rows_dev, width = tokens.shape
    slot_size = rows_dev * head_parts
    span = H // head_parts * HD
    half = width // 2
    part = width // seq_parts
    hidden_size = up_proj.shape[1]
    hidden_part = hidden_size // seq_parts
    hidden_half = hidden_part // 2

    position = jnp.argmax(dispatch_order == seq_at)
    picks = lax.dynamic_index_in_dim(random_key_blocks, position, 0, keepdims=False).reshape(-1)
    flip = head_at * (rows_dev // BLOCK_TOKENS)
    place = jnp.stack([lax.dynamic_index_in_dim(seq_lengths, seq_at, 0, keepdims=False), flip])
    place = place.astype(jnp.int32)

    own_qkv = lax.dynamic_index_in_dim(
        qkv_proj.reshape(part, 3, head_parts, span), head_at, 2, keepdims=False
    )
    vectors = jnp.concatenate([up_bias, down_bias, norm1_gain, norm1_bias, norm2_gain, norm2_bias])
    own_attn = lax.dynamic_index_in_dim(attn_proj.reshape(part, 2, half), side, 1, keepdims=False)
    attn_rows = part * half // (3 * span)
    vector_rows = -(-vectors.shape[0] // (3 * span))
    vector_rows += -vector_rows % 8
    early = jnp.concatenate(
        [
            own_qkv.reshape(part, 3 * span),
            own_attn.reshape(attn_rows, 3 * span),
            jnp.pad(vectors, (0, vector_rows * 3 * span - vectors.shape[0])).reshape(
                vector_rows, 3 * span
            ),
        ]
    )
    slot_rows = jnp.concatenate(head_gather(tokens))
    early = seq_gather(early)
    own_qkv = early[:, :part].reshape(width, 3, span)
    own_attn = early[:, part : part + attn_rows].reshape(width, half)
    vectors = early[:, part + attn_rows :].reshape(seq_parts, -1)

    def vector(start, size):
        return vectors[:, start : start + size]

    up_b = vector(0, hidden_part).reshape(seq_parts, 2, hidden_half)
    down_b, gain_one, shift_one, gain_two, shift_two = (
        vector(hidden_part + n * part, part).reshape(-1).astype(F32) for n in range(5)
    )

    up_own = lax.dynamic_index_in_dim(
        up_proj.reshape(part, seq_parts, 2, hidden_half), side, 2, keepdims=False
    ).reshape(part, hidden_size // 2)
    down_own = lax.dynamic_index_in_dim(
        down_proj.reshape(2, hidden_half, width), side, 0, keepdims=False
    )
    up_own = seq_gather(up_own).reshape(width, hidden_size // 2)
    up_other = swap(up_own, "head", 1)
    down_own = seq_gather(down_own).reshape(hidden_size // 2, width)
    down_other = swap(down_own, "head", 1)
    attn_other = swap(own_attn, "head", 1)
    attn_w = in_order(own_attn, attn_other, side, 1).reshape(width, width)
    slots = jnp.arange(head_parts) ^ head_at
    attn_w = jnp.take(attn_w.reshape(head_parts, span, width), slots, axis=0).reshape(width, width)

    queries, keys, values = (
        jnp.dot(slot_rows, own_qkv[:, n], preferred_element_type=F32).astype(BF16)
        for n in range(3)
    )
    mixed, probs, edge = attend(queries, keys, values, picks, place)
    mixed = head_exchange([mixed[k * rows_dev : (k + 1) * rows_dev] for k in range(head_parts)])
    mixed = jnp.concatenate(mixed, axis=1)
    attn_term = jnp.dot(mixed, attn_w, preferred_element_type=F32)
    resid_one = tokens.astype(F32) + attn_term
    first_norm, norm_one_back = jax.vjp(layer_norm, resid_one, gain_one, shift_one)
    first_low = first_norm.astype(BF16)

    down_term = 0.0
    kept = []
    for way, (up_w, down_w) in enumerate(((up_own, down_own), (up_other, down_other))):
        bias = lax.dynamic_index_in_dim(up_b, side ^ way, 1, keepdims=False).reshape(-1)
        up_pre = jnp.dot(first_low, up_w, preferred_element_type=F32) + bias.astype(F32)
        act, gelu_back = jax.vjp(partial(jax.nn.gelu, approximate=True), up_pre)
        act = act.astype(BF16)
        down_term = down_term + jnp.dot(act, down_w, preferred_element_type=F32)
        kept.append((act, gelu_back, up_w, down_w))
    resid_two = first_norm + down_term + down_b
    result, norm_two_back = jax.vjp(layer_norm, resid_two, gain_two, shift_two)
    grad_resid_two, grad_gain_two, grad_shift_two = norm_two_back(out_grad.astype(F32))
    grad_down_bias = jnp.sum(grad_resid_two, axis=0)
    grad_down_low = grad_resid_two.astype(BF16)

    grad_first = grad_resid_two
    down_grads, up_grads, up_bias_grads = [], [], []
    for act, gelu_back, up_w, down_w in kept:
        down_grads.append(
            jnp.einsum("tf,td->fd", act, grad_down_low, preferred_element_type=F32).astype(BF16)
        )
        grad_act = jnp.einsum("td,fd->tf", grad_down_low, down_w, preferred_element_type=F32)
        (grad_up,) = gelu_back(grad_act)
        up_bias_grads.append(jnp.sum(grad_up, axis=0))
        grad_up = grad_up.astype(BF16)
        up_grads.append(
            jnp.einsum("td,tf->df", first_low, grad_up, preferred_element_type=F32).astype(BF16)
        )
        grad_first = grad_first + jnp.einsum("tf,df->td", grad_up, up_w, preferred_element_type=F32)

    def join(own, other):
        return (own.astype(F32) + swap(other, "head", 1).astype(F32)).astype(BF16)

    def settle(total):
        total = total.astype(BF16)
        total = total.astype(F32) + swap(total, "head", 2).astype(F32)
        total = total.astype(BF16)
        return total, swap(total, "head", 1)

    down_sum = seq_reduce(join(*down_grads).reshape(seq_parts, hidden_half, width))
    up_sum = seq_reduce(join(*up_grads).reshape(seq_parts, part, hidden_size // 2))

    grad_resid_one, grad_gain_one, grad_shift_one = norm_one_back(grad_first)
    grad_attended = grad_resid_one.astype(BF16)
    grad_mixed = jnp.einsum("te,de->td", grad_attended, attn_w, preferred_element_type=F32)
    grad_mixed = grad_mixed.astype(BF16)
    grad_mixed = head_exchange(
        [grad_mixed[:, k * span : (k + 1) * span] for k in range(head_parts)]
    )
    grad_mixed = jnp.concatenate(grad_mixed)

    attn_grad = jnp.einsum("td,te->de", mixed, grad_attended, preferred_element_type=F32)
    attn_grad = jnp.take(
        attn_grad.astype(BF16).reshape(head_parts, span, width), slots, axis=0
    ).reshape(seq_parts, part, 2, half)
    up_bias_grad = in_order(
        up_bias_grads[0].reshape(seq_parts, hidden_half),
        up_bias_grads[1].reshape(seq_parts, hidden_half),
        side,
        1,
    ).reshape(seq_parts, hidden_part)
    vector_grads = jnp.concatenate(
        [up_bias_grad]
        + [
            total.reshape(seq_parts, part)
            for total in (
                grad_down_bias,
                grad_gain_one,
                grad_shift_one,
                grad_gain_two,
                grad_shift_two,
            )
        ],
        axis=1,
    ).astype(BF16)
    vector_size = vector_grads.shape[1]
    vector_rows = -(-vector_size // width)
    vector_rows += -vector_rows % 8
    vector_grads = jnp.pad(vector_grads, ((0, 0), (0, vector_rows * width - vector_size)))
    mid = jnp.concatenate([attn_grad, vector_grads.reshape(seq_parts, vector_rows, 2, half)], axis=1)
    mid_own = lax.dynamic_index_in_dim(mid, side, 2, keepdims=False)
    mid_other = lax.dynamic_index_in_dim(mid, 1 - side, 2, keepdims=False)
    mid_sum = seq_reduce(join(mid_own, mid_other))

    dq, dk, dv = attend_back(queries, keys, values, grad_mixed, probs, edge, picks, place)
    grad_packed = jnp.concatenate([dq, dk, dv], axis=1)
    grad_rows = jnp.einsum(
        "te,de->td", grad_packed, own_qkv.reshape(width, 3 * span), preferred_element_type=F32
    ).reshape(head_parts, rows_dev, width)
    sent = swap(jnp.stack([grad_rows[3], grad_rows[1]]).astype(BF16), "head", 1)
    across = swap((grad_rows[2] + sent[0].astype(F32)).astype(BF16), "head", 2)
    grad_rows = grad_resid_one + grad_rows[0] + sent[1].astype(F32) + across.astype(F32)

    qkv_grad = jnp.einsum("td,te->de", slot_rows, grad_packed, preferred_element_type=F32)
    qkv_sum = seq_reduce(qkv_grad.astype(BF16).reshape(seq_parts, part, 3 * span))
    qkv_sum = jnp.stack(head_gather(qkv_sum.astype(BF16)))
    qkv_sum = jnp.take(qkv_sum, slots, axis=0).reshape(head_parts, part, 3, span)
    qkv_sum = qkv_sum.transpose(1, 2, 0, 3).reshape(part, 3 * width).astype(F32)

    down_sum = in_order(*settle(down_sum), side, 0).reshape(hidden_part, width).astype(F32)
    up_sum = in_order(
        *(each.reshape(part, seq_parts, hidden_half) for each in settle(up_sum)), side, 2
    )
    up_sum = up_sum.reshape(part, hidden_size).astype(F32)
    mid_sum = in_order(*settle(mid_sum), side, 1).reshape(part + vector_rows, width).astype(F32)
    vector_sum = mid_sum[part:].reshape(-1)

    def owned(n):
        return vector_sum[hidden_part + n * part : hidden_part + (n + 1) * part]

    return (
        result.astype(BF16),
        grad_rows.astype(BF16),
        qkv_sum,
        mid_sum[:part],
        up_sum,
        vector_sum[:hidden_part],
        down_sum,
        owned(0),
        owned(1),
        owned(2),
        owned(3),
        owned(4),
    )


def solution(mesh):
    rows = P(("seq", "head"), None)
    matrix, flat = P("seq", None), P("seq")
    return jax.shard_map(
        on_device,
        mesh=mesh,
        in_specs=(rows, rows, P(), P(), P(), matrix, matrix, matrix, flat, matrix)
        + (flat,) * 5,
        out_specs=(rows, rows, matrix, matrix, matrix, flat, matrix) + (flat,) * 5,
        check_vma=False,
    )
```
